32 devices in a mesh: chain: 8 (over y, x, core), cross: 4 (over z).
Axes of the slice: x: 2, y: 2, z: 4, core: 2. Of those that a mesh axis runs over, the one named last changes fastest.
Arguments:
- moments: float32 [20, 512, 1024], P(None, 'cross', 'chain'), as said below
- flags: int32 [512, 1024], P('cross', 'chain'), may hold values from 0 to 2
- shifts: int32 [512, 8], P('cross', 'chain'), may hold values from -48 to 48
- fraction: float32 [512], P('cross'), may hold values from 0.05 to 0.95
Outputs:
- remapped: float32 [20, 512, 1024], P(None, 'cross', 'chain')
- mass_coord: float32 [5, 512, 1024], P(None, 'cross', 'chain')
The draws below stay inside these ranges and needn't reach their ends.
Inputs may be any that keep to these rules, and one draw needn't show every extreme that they name: zeroth-order moments are positive.
All inputs are finite; a program needn't handle non-finite values.
Results may differ from the reference program's by a relative error of at most 0.000084.
Values sent between devices are 32-bit elements; how exact they have to be, the bound alone decides.
A program may use at most 128 MiB of HBM per device.

```python
import jax
import jax.numpy as jnp
from jax import lax

VARS = 5
MOMENTS = 4
BLOCK = 128
SHIFT_MAX = 48
NX = 1024
PENCILS = 512
NBLK = 8


def draw_moments(key, part):
    key_base, key_high = jax.random.split(jax.random.fold_in(key, 7))
    rise_x = 1.0 + 2.0 * jnp.arange(NX, dtype=jnp.float32) / NX
    rise_p = 1.0 + 2.0 * jnp.arange(PENCILS, dtype=jnp.float32) / PENCILS
    scale = rise_p[:, None] * rise_x[None, :]
    base = jax.random.uniform(key_base, (VARS, PENCILS, NX), jnp.float32, 0.15, 0.6)
    higher = jax.random.normal(key_high, (VARS, MOMENTS - 1, PENCILS, NX), jnp.float32)
    means = base * scale[None]
    coefficients = jnp.array([0.5, 0.25, 0.12], jnp.float32)[None, :, None, None]
    rest = higher * coefficients * means[:, None]
    whole = jnp.concatenate([means[:, None], rest], axis=1)
    return whole.reshape(VARS * MOMENTS, PENCILS, NX).astype(jnp.float32)


def plant(values, key, low, top_value):
    longest = values.shape.index(max(values.shape))
    spots = []
    for shift in (0, 1):
        where = [jax.random.randint(jax.random.fold_in(key, axis), (), 0, length) for axis, length in enumerate(values.shape)]
        where[longest] = (where[longest] + shift) % values.shape[longest]
        spots.append(tuple(where))
    return values.at[spots[0]].set(low).at[spots[1]].set(top_value)


def block_scale(own_key, dims, shards, least, top_value):
    factor_of = 1.0
    for dim, blocks in shards:
        draws = jax.random.uniform(jax.random.fold_in(jax.random.fold_in(own_key, 6), dim), (blocks,), jnp.float32, least / len(shards), top_value / len(shards))
        factor_of = factor_of * jnp.repeat(jnp.exp(draws), dims[dim] // blocks).reshape((-1,) + (1,) * (len(dims) - 1 - dim))
    return factor_of


def setup_inputs(seed: int = 0) -> dict:
    keys = jax.random.split(jax.random.key(seed), 5)
    return {
        "moments": draw_moments(jax.random.fold_in(keys[4], 71), 0),
        "flags": plant(jax.random.randint(keys[1], (PENCILS, NX), 0, 3), jax.random.fold_in(keys[1], 1), 0, 2).astype(jnp.int32),
        "shifts": plant(jax.random.randint(keys[2], (PENCILS, NBLK), 0 - SHIFT_MAX, SHIFT_MAX + 1), jax.random.fold_in(keys[2], 1), 0 - SHIFT_MAX, SHIFT_MAX).astype(jnp.int32),
        "fraction": jnp.clip(0.05 + 0.9 * jax.random.uniform(keys[3], (PENCILS,), jnp.float32) ** block_scale(keys[3], (PENCILS,), ((0, 4),), -0.2, 0.2), 0.05, 0.95),
    }


gauss_nodes = (-0.8611363115940526, -0.3399810435848563, 0.3399810435848563, 0.8611363115940526)
gauss_weights = (0.3478548451374538, 0.6521451548625461, 0.6521451548625461, 0.3478548451374538)


def legendre_values(point):
    return [jnp.ones_like(point), point, 0.5 * (3.0 * point * point - 1.0), 0.5 * (5.0 * point * point * point - 3.0 * point)]


def interval_matrix(low_end, high_end, offset):
    half = 0.5 * (high_end - low_end)
    middle = 0.5 * (high_end + low_end)
    entries = [[jnp.zeros_like(low_end) for source_order in range(4)] for target_order in range(4)]
    for node, weight in zip(gauss_nodes, gauss_weights):
        point = middle + half * node
        target = legendre_values(point)
        source = legendre_values(point + offset)
        for target_order in range(4):
            for source_order in range(4):
                entries[target_order][source_order] = entries[target_order][source_order] + weight * half * target[target_order] * source[source_order]
    return jnp.stack([jnp.stack([(target_order + 0.5) * entries[target_order][source_order] for source_order in range(4)]) for target_order in range(4)])


def remap_matrices(fraction):
    first = interval_matrix(-1.0 + 0.0 * fraction, 1.0 - 2.0 * fraction, 2.0 * fraction)
    second = interval_matrix(1.0 - 2.0 * fraction, 1.0 + 0.0 * fraction, 2.0 * fraction - 2.0)
    return first, second


def partial_weights(fraction):
    shifted = 2.0 * fraction - 1.0
    square = shifted * shifted
    return jnp.stack([fraction, fraction * fraction - fraction, 0.25 * (square * shifted - shifted), 0.5 * (0.5 * (1.25 * square * square - 1.5 * square) + 0.125)])


def keep_mask(flags):
    order = jnp.arange(4, dtype=jnp.int32)[:, None, None]
    keep = (order == 0) | ((order == 1) & (flags[None] <= 1)) | (flags[None] == 0)
    return keep.astype(jnp.float32)


def reference(moments, flags, shifts, fraction):
    halo_width = SHIFT_MAX + 1
    expanded = moments.reshape(VARS, MOMENTS, PENCILS, NX)
    limited = expanded * keep_mask(flags)[None]
    padded = jnp.pad(limited, ((0, 0), (0, 0), (0, 0), (halo_width, halo_width)))
    cell_shift = jnp.repeat(shifts, BLOCK, axis=1)
    source = (jnp.arange(NX, dtype=jnp.int32)[None, :] + cell_shift + halo_width).astype(jnp.int32)
    source_cells = jnp.take_along_axis(padded, source[None, None], axis=3)
    next_cells = jnp.take_along_axis(padded, (source + 1)[None, None], axis=3)
    first, second = remap_matrices(fraction)
    remapped = jnp.einsum("kmp,vmpc->vkpc", first, source_cells, precision=lax.Precision.HIGHEST)
    remapped = remapped + jnp.einsum("kmp,vmpc->vkpc", second, next_cells, precision=lax.Precision.HIGHEST)
    means = padded[:, 0]
    cum = jnp.cumsum(means, axis=-1) - means
    cum_at = jnp.take_along_axis(cum, source[None], axis=2)
    partial_value = jnp.einsum("vmpc,mp->vpc", source_cells, partial_weights(fraction), precision=lax.Precision.HIGHEST)
    grand_sum = jnp.sum(expanded[:, 0], axis=(1, 2))
    mass_coord = (cum_at + partial_value) / (grand_sum / PENCILS)[:, None, None]
    return remapped.reshape(VARS * MOMENTS, PENCILS, NX), mass_coord
```

```python
import functools

import jax
import jax.numpy as jnp
from jax import lax
from jax.experimental import pallas as pl
from jax.experimental.pallas import tpu as pltpu
from jax.sharding import PartitionSpec as P

VARS = 5
MOMENTS = 4
BLOCK = 128
SHIFT_MAX = 48
ROWS = VARS * MOMENTS
STRIDE = SHIFT_MAX + 1
CHUNKS = -(-ROWS * STRIDE // BLOCK)
GROUP = 8
COEFS = 2 * MOMENTS * MOMENTS + MOMENTS
MESH = pl.DeviceIdType.MESH
HIGHEST = lax.Precision.HIGHEST

gauss_nodes = (-0.8611363115940526, -0.3399810435848563, 0.3399810435848563, 0.8611363115940526)
gauss_weights = (0.3478548451374538, 0.6521451548625461, 0.6521451548625461, 0.3478548451374538)


def segments(first, length):
    held = [[] for _ in range(CHUNKS)]
    for row in range(ROWS):
        start = first + STRIDE * row
        chunk, lane = divmod(start, BLOCK)
        held[chunk % CHUNKS].append((lane, row))
        if lane + length > BLOCK:
            held[(chunk + 1) % CHUNKS].append((0, row))
    return [sorted(chunk) for chunk in held]


AFTER_FIRST, AFTER_LENGTH = SHIFT_MAX, SHIFT_MAX + 1
BEFORE_FIRST, BEFORE_LENGTH = 0, SHIFT_MAX
AFTER = segments(AFTER_FIRST, AFTER_LENGTH)
BEFORE = segments(BEFORE_FIRST, BEFORE_LENGTH)


def places(row, first, length):
    chunk, lane = divmod(first + STRIDE * row, BLOCK)
    chunks = [chunk % CHUNKS]
    if lane + length > BLOCK:
        chunks.append((chunk + 1) % CHUNKS)
    return chunks, lane


def last_chunk(var):
    need = [0]
    for row in range(MOMENTS * var, MOMENTS * (var + 1)):
        need += places(row, AFTER_FIRST, AFTER_LENGTH)[0]
        need += places(row, BEFORE_FIRST, BEFORE_LENGTH)[0]
    return max(need)


def legendre_values(point):
    return [
        jnp.ones_like(point),
        point,
        0.5 * (3.0 * point * point - 1.0),
        0.5 * (5.0 * point * point * point - 3.0 * point),
    ]


def interval_matrix(low_end, high_end, offset):
    half = 0.5 * (high_end - low_end)
    middle = 0.5 * (high_end + low_end)
    entries = [[jnp.zeros_like(low_end) for _ in range(4)] for _ in range(4)]
    for node, weight in zip(gauss_nodes, gauss_weights):
        point = middle + half * node
        target = legendre_values(point)
        source = legendre_values(point + offset)
        for k in range(4):
            scaled = weight * half * target[k]
            for m in range(4):
                entries[k][m] = entries[k][m] + scaled * source[m]
    return [(k + 0.5) * entries[k][m] for k in range(4) for m in range(4)]


def partial_weights(fraction):
    shifted = 2.0 * fraction - 1.0
    square = shifted * shifted
    return [
        fraction,
        fraction * fraction - fraction,
        0.25 * (square * shifted - shifted),
        0.5 * (0.5 * (1.25 * square * square - 1.5 * square) + 0.125),
    ]


def kernel(
    chain, cross,
    moments, flags, shifts, fraction,
    remapped, mass,
    to_left, to_right, from_left, from_right,
    sums, parts, raw, coef, carried, shift_of, mean_of, window,
    left_send, left_recv, right_send, right_recv,
    sum_send, sum_recv, part_send, part_recv,
):
    pencils = moments.shape[1]
    groups = pencils // GROUP
    me = lax.axis_index("chain")
    plane = lax.axis_index("cross")

    barrier = pltpu.get_barrier_semaphore()
    for step in range(1, chain):
        peer = lax.rem(me + step, chain)
        pl.semaphore_signal(barrier, inc=1, device_id={"chain": peer}, device_id_type=MESH)
    for step in range(1, cross):
        peer = lax.rem(plane + step, cross)
        pl.semaphore_signal(barrier, inc=1, device_id={"cross": peer}, device_id_type=MESH)

    row_id = lax.broadcasted_iota(jnp.int32, (8, BLOCK), 0)
    total = jnp.zeros((8, pencils), jnp.float32)
    for var in range(VARS):
        pick = (row_id == var).astype(jnp.float32)
        total = total + lax.dot_general(
            pick, moments[MOMENTS * var], (((1,), (1,)), ((), ())),
            precision=HIGHEST, preferred_element_type=jnp.float32,
        )
    sums[me] = total

    lane = lax.broadcasted_iota(jnp.int32, (GROUP, BLOCK), 1)

    def limited_row(row, rows, keep_linear, keep_full):
        value = moments[row, rows, :]
        order = row % MOMENTS
        if order == 1:
            value = jnp.where(keep_linear, value, 0.0)
        elif order > 1:
            value = jnp.where(keep_full, value, 0.0)
        return value

    def pack(group, carry):
        rows = pl.ds(pl.multiple_of(group * GROUP, GROUP), GROUP)
        flag = flags[rows, :]
        keep_linear, keep_full = flag <= 1, flag == 0
        rolled = [
            pltpu.roll(
                limited_row(row, rows, keep_linear, keep_full),
                (STRIDE * row + SHIFT_MAX) % BLOCK, 1,
            )
            for row in range(ROWS)
        ]
        for chunk in range(CHUNKS):
            for held, target in ((AFTER, to_left), (BEFORE, to_right)):
                value = rolled[held[chunk][0][1]]
                for start, row in held[chunk][1:]:
                    value = jnp.where(lane >= start, rolled[row], value)
                target[chunk, rows, :] = value
        return carry

    lax.fori_loop(0, groups, pack, 0)

    pl.semaphore_wait(barrier, chain - 1 + cross - 1)

    sum_copies = []
    for step in range(1, chain):
        copy = pltpu.make_async_remote_copy(
            src_ref=sums.at[me], dst_ref=sums.at[me],
            send_sem=sum_send.at[step], recv_sem=sum_recv.at[step],
            device_id={"chain": lax.rem(me + step, chain)}, device_id_type=MESH,
        )
        copy.start()
        sum_copies.append(copy)

    def leftward(chunk):
        return pltpu.make_async_remote_copy(
            src_ref=to_left.at[chunk], dst_ref=from_right.at[chunk],
            send_sem=left_send.at[chunk], recv_sem=left_recv.at[chunk],
            device_id={"chain": lax.rem(me + chain - 1, chain)}, device_id_type=MESH,
        )

    def rightward(chunk):
        return pltpu.make_async_remote_copy(
            src_ref=to_right.at[chunk], dst_ref=from_left.at[chunk],
            send_sem=right_send.at[chunk], recv_sem=right_recv.at[chunk],
            device_id={"chain": lax.rem(me + 1, chain)}, device_id_type=MESH,
        )

    has_left, has_right = me > 0, me < chain - 1

    @pl.when(has_left)
    def _():
        for chunk in range(CHUNKS):
            leftward(chunk).start()

    @pl.when(has_right)
    def _():
        for chunk in range(CHUNKS):
            rightward(chunk).start()

    @pl.when(me == 0)
    def _():
        from_left[...] = jnp.zeros_like(from_left)

    @pl.when(me == chain - 1)
    def _():
        from_right[...] = jnp.zeros_like(from_right)

    f = fraction[...]
    first = interval_matrix(-1.0 + 0.0 * f, 1.0 - 2.0 * f, 2.0 * f)
    second = interval_matrix(1.0 - 2.0 * f, 1.0 + 0.0 * f, 2.0 * f - 2.0)
    raw[...] = jnp.zeros_like(raw)
    columns = first + second + partial_weights(f) + [shifts[...].astype(jnp.float32)]
    for index, value in enumerate(columns):
        raw[index : index + 1, :] = value
    turned = jnp.transpose(raw[...])
    for index in range(COEFS):
        coef[index] = jnp.broadcast_to(turned[:, index : index + 1], (pencils, BLOCK))
    shift_of[...] = jnp.broadcast_to(turned[:, COEFS : COEFS + 1], (pencils, BLOCK)).astype(jnp.int32)

    for copy in sum_copies:
        copy.wait_recv()
    before = jnp.zeros((8, pencils), jnp.float32)
    whole = jnp.zeros((8, pencils), jnp.float32)
    for index in range(chain):
        value = sums[index]
        before = before + jnp.where(index < me, value, 0.0)
        whole = whole + value
    parts[plane] = jnp.broadcast_to(jnp.sum(whole, axis=1, keepdims=True), (8, BLOCK))
    part_copies = []
    for step in range(1, cross):
        copy = pltpu.make_async_remote_copy(
            src_ref=parts.at[plane], dst_ref=parts.at[plane],
            send_sem=part_send.at[step], recv_sem=part_recv.at[step],
            device_id={"cross": lax.rem(plane + step, cross)}, device_id_type=MESH,
        )
        copy.start()
        part_copies.append(copy)
    raw[0:8, :] = before
    turned = jnp.transpose(raw[...])
    for var in range(VARS):
        carried[var] = jnp.broadcast_to(turned[:, var : var + 1], (pencils, BLOCK))
    for copy in part_copies:
        copy.wait_recv()
    grand = parts[0]
    for index in range(1, cross):
        grand = grand + parts[index]
    mean_of[...] = grand / float(pencils * cross)

    source_cell = lax.broadcasted_iota(jnp.int32, (2 * BLOCK, BLOCK), 0)
    target_cell = lax.broadcasted_iota(jnp.int32, (2 * BLOCK, BLOCK), 1)
    triangle = jnp.where((source_cell < target_cell) | (source_cell >= BLOCK), 1.0, 0.0)

    def halo_row(row, rows, ahead):
        values = []
        for ref, first_lane, length in (
            (from_right, AFTER_FIRST, AFTER_LENGTH),
            (from_left, BEFORE_FIRST, BEFORE_LENGTH),
        ):
            chunks, start = places(row, first_lane, length)
            value = ref[chunks[0], rows, :]
            if len(chunks) > 1:
                value = jnp.where(lane >= start, value, ref[chunks[1], rows, :])
            values.append(value)
        value = jnp.where(ahead, values[0], values[1])
        return pltpu.roll(value, (-(STRIDE * row + SHIFT_MAX)) % BLOCK, 1)

    ready = 0
    for var in range(VARS):
        needed = last_chunk(var) + 1
        if needed > ready:
            low, ready = ready, needed

            @pl.when(has_right)
            def _(low=low, high=needed):
                for chunk in range(low, high):
                    leftward(chunk).wait_recv()

            @pl.when(has_left)
            def _(low=low, high=needed):
                for chunk in range(low, high):
                    rightward(chunk).wait_recv()

        def remap(group, carry, var=var):
            rows = pl.ds(pl.multiple_of(group * GROUP, GROUP), GROUP)
            flag = flags[rows, :]
            keep_linear, keep_full = flag <= 1, flag == 0
            shift = shift_of[rows, :]
            ahead = shift >= 0
            turn = shift & (BLOCK - 1)
            outside = jnp.where(ahead, lane - turn, turn - 1 - lane) < 0
            outside_next = jnp.where(ahead, lane - turn - 1, turn - lane) < 0
            at = (lane + turn) & (BLOCK - 1)
            at_next = (lane + turn + 1) & (BLOCK - 1)
            here, beyond = [], []
            for order in range(MOMENTS):
                row = MOMENTS * var + order
                own = limited_row(row, rows, keep_linear, keep_full)
                halo = halo_row(row, rows, ahead)
                here.append(
                    jnp.take_along_axis(
                        jnp.where(outside, halo, own), at, axis=1, mode="promise_in_bounds"
                    )
                )
                beyond.append(
                    jnp.take_along_axis(
                        jnp.where(outside_next, halo, own), at_next, axis=1, mode="promise_in_bounds"
                    )
                )
                if order == 0:
                    gap = jnp.where(outside, jnp.where(ahead, own, -halo), 0.0)
            window[rows, 0:BLOCK] = here[0]
            window[rows, BLOCK : 2 * BLOCK] = gap
            for k in range(MOMENTS):
                value = None
                for m in range(MOMENTS):
                    term = coef[MOMENTS * k + m, rows, :] * here[m]
                    value = term if value is None else value + term
                    value = value + coef[MOMENTS * (MOMENTS + k) + m, rows, :] * beyond[m]
                remapped[MOMENTS * var + k, rows, :] = value
            value = coef[2 * MOMENTS * MOMENTS, rows, :] * here[0]
            for m in range(1, MOMENTS):
                value = value + coef[2 * MOMENTS * MOMENTS + m, rows, :] * here[m]
            mass[var, rows, :] = value + carried[var, rows, :]
            return carry

        lax.fori_loop(0, groups, remap, 0)
        summed = jnp.dot(
            window[...], triangle, precision=HIGHEST, preferred_element_type=jnp.float32
        )
        mass[var] = (summed + mass[var]) / mean_of[var : var + 1, :]

    for copy in sum_copies + part_copies:
        copy.wait_send()

    @pl.when(has_left)
    def _():
        for chunk in range(CHUNKS):
            leftward(chunk).wait_send()

    @pl.when(has_right)
    def _():
        for chunk in range(CHUNKS):
            rightward(chunk).wait_send()


def solution(mesh):
    chain, cross = mesh.shape["chain"], mesh.shape["cross"]

    def shards(moments, flags, shifts, fraction):
        row_count, pencils, cells = moments.shape
        assert row_count == ROWS and cells == BLOCK and pencils == BLOCK
        chunk = pltpu.VMEM((CHUNKS, pencils, BLOCK), jnp.float32)
        dma = pltpu.SemaphoreType.DMA
        return pl.pallas_call(
            functools.partial(kernel, chain, cross),
            out_shape=(
                jax.ShapeDtypeStruct(moments.shape, jnp.float32),
                jax.ShapeDtypeStruct((VARS, pencils, cells), jnp.float32),
            ),
            in_specs=[pl.BlockSpec(memory_space=pltpu.VMEM)] * 4,
            out_specs=(pl.BlockSpec(memory_space=pltpu.VMEM),) * 2,
            scratch_shapes=[
                chunk, chunk, chunk, chunk,
                pltpu.VMEM((chain, 8, pencils), jnp.float32),
                pltpu.VMEM((cross, 8, BLOCK), jnp.float32),
                pltpu.VMEM((BLOCK, pencils), jnp.float32),
                pltpu.VMEM((COEFS, pencils, BLOCK), jnp.float32),
                pltpu.VMEM((VARS, pencils, BLOCK), jnp.float32),
                pltpu.VMEM((pencils, BLOCK), jnp.int32),
                pltpu.VMEM((8, BLOCK), jnp.float32),
                pltpu.VMEM((pencils, 2 * BLOCK), jnp.float32),
                dma((CHUNKS,)), dma((CHUNKS,)), dma((CHUNKS,)), dma((CHUNKS,)),
                dma((chain,)), dma((chain,)), dma((cross,)), dma((cross,)),
            ],
            compiler_params=pltpu.CompilerParams(
                collective_id=0, has_side_effects=True, vmem_limit_bytes=48 << 20
            ),
        )(moments, flags, shifts.T, fraction.reshape(1, pencils))

    in_specs = (P(None, "cross", "chain"), P("cross", "chain"), P("cross", "chain"), P("cross"))
    out_specs = (P(None, "cross", "chain"), P(None, "cross", "chain"))
    return jax.shard_map(shards, mesh=mesh, in_specs=in_specs, out_specs=out_specs, check_vma=False)
```

```python
import functools

import jax
import jax.numpy as jnp
from jax import lax
from jax.experimental import pallas as pl
from jax.experimental.pallas import tpu as pltpu
from jax.sharding import PartitionSpec as P

VARS = 5
MOMENTS = 4
BLOCK = 128
SHIFT_MAX = 48
ROWS = VARS * MOMENTS
STRIDE = SHIFT_MAX + 1
CHUNKS = -(-ROWS * STRIDE // BLOCK)
GROUP = 64
SEND_SUMS = 2
SUMS_AT = 3
COEFS = 2 * MOMENTS * MOMENTS + MOMENTS
MESH = pl.DeviceIdType.MESH
HIGHEST = lax.Precision.HIGHEST

gauss_nodes = (-0.8611363115940526, -0.3399810435848563, 0.3399810435848563, 0.8611363115940526)
gauss_weights = (0.3478548451374538, 0.6521451548625461, 0.6521451548625461, 0.3478548451374538)


def segments(first, length):
    held = [[] for _ in range(CHUNKS)]
    for row in range(ROWS):
        start = first + STRIDE * row
        chunk, lane = divmod(start, BLOCK)
        held[chunk % CHUNKS].append((lane, row))
        if lane + length > BLOCK:
            held[(chunk + 1) % CHUNKS].append((0, row))
    return [sorted(chunk) for chunk in held]


AFTER_FIRST, AFTER_LENGTH = SHIFT_MAX, SHIFT_MAX + 1
BEFORE_FIRST, BEFORE_LENGTH = 0, SHIFT_MAX
AFTER = segments(AFTER_FIRST, AFTER_LENGTH)
BEFORE = segments(BEFORE_FIRST, BEFORE_LENGTH)


def places(row, first, length):
    chunk, lane = divmod(first + STRIDE * row, BLOCK)
    chunks = [chunk % CHUNKS]
    if lane + length > BLOCK:
        chunks.append((chunk + 1) % CHUNKS)
    return chunks, lane


def last_chunk(var):
    need = [0]
    for row in range(MOMENTS * var, MOMENTS * (var + 1)):
        need += places(row, AFTER_FIRST, AFTER_LENGTH)[0]
        need += places(row, BEFORE_FIRST, BEFORE_LENGTH)[0]
    return max(need)


def legendre_values(point):
    return [
        jnp.ones_like(point),
        point,
        0.5 * (3.0 * point * point - 1.0),
        0.5 * (5.0 * point * point * point - 3.0 * point),
    ]


def interval_matrix(low_end, high_end, offset):
    half = 0.5 * (high_end - low_end)
    middle = 0.5 * (high_end + low_end)
    entries = [[jnp.zeros_like(low_end) for _ in range(4)] for _ in range(4)]
    for node, weight in zip(gauss_nodes, gauss_weights):
        point = middle + half * node
        target = legendre_values(point)
        source = legendre_values(point + offset)
        for k in range(4):
            scaled = weight * half * target[k]
            for m in range(4):
                entries[k][m] = entries[k][m] + scaled * source[m]
    return [(k + 0.5) * entries[k][m] for k in range(4) for m in range(4)]


def partial_weights(fraction):
    shifted = 2.0 * fraction - 1.0
    square = shifted * shifted
    return [
        fraction,
        fraction * fraction - fraction,
        0.25 * (square * shifted - shifted),
        0.5 * (0.5 * (1.25 * square * square - 1.5 * square) + 0.125),
    ]


def kernel(
    chain, cross,
    moments_in, flags_in, shifts_in, fraction_in,
    remapped, mass,
    moments, flags, shifts, fraction,
    to_left, to_right, from_left, from_right,
    sums, parts, raw, coef, carried, shift_of, mean_of, window,
    left_send, left_recv, right_send, right_recv,
    sum_send, sum_recv, part_send, part_recv, input_sem,
):
    pencils = moments.shape[1]
    groups = pencils // GROUP
    me = lax.axis_index("chain")
    plane = lax.axis_index("cross")

    inputs = [
        pltpu.make_async_copy(source, target, input_sem.at[index])
        for index, (source, target) in enumerate(
            ((moments_in, moments), (flags_in, flags), (shifts_in, shifts), (fraction_in, fraction))
        )
    ]
    for copy in inputs:
        copy.start()

    barrier = pltpu.get_barrier_semaphore()
    for step in range(1, chain):
        peer = lax.rem(me + step, chain)
        pl.semaphore_signal(barrier, inc=1, device_id={"chain": peer}, device_id_type=MESH)
    for step in range(1, cross):
        peer = lax.rem(plane + step, cross)
        pl.semaphore_signal(barrier, inc=1, device_id={"cross": peer}, device_id_type=MESH)

    for copy in inputs:
        copy.wait()

    lane = lax.broadcasted_iota(jnp.int32, (GROUP, BLOCK), 1)

    def limited_row(row, rows, keep_linear, keep_full):
        value = moments[row, rows, :]
        order = row % MOMENTS
        if order == 1:
            value = jnp.where(keep_linear, value, 0.0)
        elif order > 1:
            value = jnp.where(keep_full, value, 0.0)
        return value

    def leftward(chunk):
        return pltpu.make_async_remote_copy(
            src_ref=to_left.at[chunk], dst_ref=from_right.at[chunk],
            send_sem=left_send.at[chunk], recv_sem=left_recv.at[chunk],
            device_id={"chain": lax.rem(me + chain - 1, chain)}, device_id_type=MESH,
        )

    def rightward(chunk):
        return pltpu.make_async_remote_copy(
            src_ref=to_right.at[chunk], dst_ref=from_left.at[chunk],
            send_sem=right_send.at[chunk], recv_sem=right_recv.at[chunk],
            device_id={"chain": lax.rem(me + 1, chain)}, device_id_type=MESH,
        )

    has_left, has_right = me > 0, me < chain - 1

    sum_copies = [
        pltpu.make_async_remote_copy(
            src_ref=sums.at[me], dst_ref=sums.at[me],
            send_sem=sum_send.at[step], recv_sem=sum_recv.at[step],
            device_id={"chain": lax.rem(me + step, chain)}, device_id_type=MESH,
        )
        for step in range(1, chain)
    ]

    def send_sums():
        row_id = lax.broadcasted_iota(jnp.int32, (8, BLOCK), 0)
        total = jnp.zeros((8, pencils), jnp.float32)
        for var in range(VARS):
            pick = (row_id == var).astype(jnp.float32)
            total = total + lax.dot_general(
                pick, moments[MOMENTS * var], (((1,), (1,)), ((), ())),
                precision=HIGHEST, preferred_element_type=jnp.float32,
            )
        sums[me] = total
        for copy in sum_copies:
            copy.start()

    def pack(chunk):
        def body(group, carry):
            rows = pl.ds(pl.multiple_of(group * GROUP, GROUP), GROUP)
            flag = flags[rows, :]
            keep_linear, keep_full = flag <= 1, flag == 0
            rolled = {
                row: pltpu.roll(
                    limited_row(row, rows, keep_linear, keep_full),
                    (STRIDE * row + SHIFT_MAX) % BLOCK, 1,
                )
                for row in sorted({row for held in (AFTER, BEFORE) for _, row in held[chunk]})
            }
            for held, target in ((AFTER, to_left), (BEFORE, to_right)):
                value = rolled[held[chunk][0][1]]
                for start, row in held[chunk][1:]:
                    value = jnp.where(lane >= start, rolled[row], value)
                target[chunk, rows, :] = value
            return carry

        lax.fori_loop(0, groups, body, 0)

    for chunk in range(CHUNKS):
        pack(chunk)
        if chunk == 0:
            pl.semaphore_wait(barrier, chain - 1 + cross - 1)

        @pl.when(has_left)
        def _(chunk=chunk):
            leftward(chunk).start()

        @pl.when(has_right)
        def _(chunk=chunk):
            rightward(chunk).start()

        if chunk == SEND_SUMS - 1:
            send_sums()

    @pl.when(me == 0)
    def _():
        from_left[...] = jnp.zeros_like(from_left)

    @pl.when(me == chain - 1)
    def _():
        from_right[...] = jnp.zeros_like(from_right)

    f = fraction[...]
    first = interval_matrix(-1.0 + 0.0 * f, 1.0 - 2.0 * f, 2.0 * f)
    second = interval_matrix(1.0 - 2.0 * f, 1.0 + 0.0 * f, 2.0 * f - 2.0)
    raw[...] = jnp.zeros_like(raw)
    columns = first + second + partial_weights(f) + [shifts[...].astype(jnp.float32)]
    for index, value in enumerate(columns):
        raw[index : index + 1, :] = value
    turned = jnp.transpose(raw[...])
    for index in range(COEFS):
        coef[index] = jnp.broadcast_to(turned[:, index : index + 1], (pencils, BLOCK))
    shift_of[...] = jnp.broadcast_to(turned[:, COEFS : COEFS + 1], (pencils, BLOCK)).astype(jnp.int32)

    source_cell = lax.broadcasted_iota(jnp.int32, (2 * BLOCK, BLOCK), 0)
    target_cell = lax.broadcasted_iota(jnp.int32, (2 * BLOCK, BLOCK), 1)
    triangle = jnp.where((source_cell < target_cell) | (source_cell >= BLOCK), 1.0, 0.0)

    def halo_row(row, rows, ahead):
        values = []
        for ref, first_lane, length in (
            (from_right, AFTER_FIRST, AFTER_LENGTH),
            (from_left, BEFORE_FIRST, BEFORE_LENGTH),
        ):
            chunks, start = places(row, first_lane, length)
            value = ref[chunks[0], rows, :]
            if len(chunks) > 1:
                value = jnp.where(lane >= start, value, ref[chunks[1], rows, :])
            values.append(value)
        value = jnp.where(ahead, values[0], values[1])
        return pltpu.roll(value, (-(STRIDE * row + SHIFT_MAX)) % BLOCK, 1)

    part_copies = [
        pltpu.make_async_remote_copy(
            src_ref=parts.at[plane], dst_ref=parts.at[plane],
            send_sem=part_send.at[step], recv_sem=part_recv.at[step],
            device_id={"cross": lax.rem(plane + step, cross)}, device_id_type=MESH,
        )
        for step in range(1, cross)
    ]

    def reduce_chain():
        for copy in sum_copies:
            copy.wait_recv()
        before = jnp.zeros((8, pencils), jnp.float32)
        whole = jnp.zeros((8, pencils), jnp.float32)
        for index in range(chain):
            value = sums[index]
            before = before + jnp.where(index < me, value, 0.0)
            whole = whole + value
        parts[plane] = jnp.broadcast_to(jnp.sum(whole, axis=1, keepdims=True), (8, BLOCK))
        for copy in part_copies:
            copy.start()
        raw[0:8, :] = before
        turned = jnp.transpose(raw[...])
        for var in range(VARS):
            carried[var] = jnp.broadcast_to(turned[:, var : var + 1], (pencils, BLOCK))

    def finish_sums():
        for copy in part_copies:
            copy.wait_recv()
        grand = parts[0]
        for index in range(1, cross):
            grand = grand + parts[index]
        mean_of[...] = grand / float(pencils * cross)

    def finish(var):
        mass[var] = (mass[var] + carried[var]) / mean_of[var : var + 1, :]

    ready = 0
    for var in range(VARS):
        if var == SUMS_AT:
            reduce_chain()
        if var == VARS - 1:
            finish_sums()
            for done in range(VARS - 1):
                finish(done)

        needed = last_chunk(var) + 1
        if needed > ready:
            low, ready = ready, needed

            @pl.when(has_right)
            def _(low=low, high=needed):
                for chunk in range(low, high):
                    leftward(chunk).wait_recv()

            @pl.when(has_left)
            def _(low=low, high=needed):
                for chunk in range(low, high):
                    rightward(chunk).wait_recv()

        def remap(group, carry, var=var):
            rows = pl.ds(pl.multiple_of(group * GROUP, GROUP), GROUP)
            flag = flags[rows, :]
            keep_linear, keep_full = flag <= 1, flag == 0
            shift = shift_of[rows, :]
            ahead = shift >= 0
            turn = shift & (BLOCK - 1)
            outside = jnp.where(ahead, lane - turn, turn - 1 - lane) < 0
            outside_next = jnp.where(ahead, lane - turn - 1, turn - lane) < 0
            at = (lane + turn) & (BLOCK - 1)
            at_next = (lane + turn + 1) & (BLOCK - 1)
            here, beyond = [], []
            for order in range(MOMENTS):
                row = MOMENTS * var + order
                own = limited_row(row, rows, keep_linear, keep_full)
                halo = halo_row(row, rows, ahead)
                here.append(
                    jnp.take_along_axis(
                        jnp.where(outside, halo, own), at, axis=1, mode="promise_in_bounds"
                    )
                )
                beyond.append(
                    jnp.take_along_axis(
                        jnp.where(outside_next, halo, own), at_next, axis=1, mode="promise_in_bounds"
                    )
                )
                if order == 0:
                    gap = jnp.where(outside, jnp.where(ahead, own, -halo), 0.0)
            window[rows, 0:BLOCK] = here[0]
            window[rows, BLOCK : 2 * BLOCK] = gap
            for k in range(MOMENTS):
                value = None
                for m in range(MOMENTS):
                    term = coef[MOMENTS * k + m, rows, :] * here[m]
                    value = term if value is None else value + term
                    value = value + coef[MOMENTS * (MOMENTS + k) + m, rows, :] * beyond[m]
                remapped[MOMENTS * var + k, rows, :] = value
            value = coef[2 * MOMENTS * MOMENTS, rows, :] * here[0]
            for m in range(1, MOMENTS):
                value = value + coef[2 * MOMENTS * MOMENTS + m, rows, :] * here[m]
            mass[var, rows, :] = value
            return carry

        lax.fori_loop(0, groups, remap, 0)
        summed = jnp.dot(
            window[...], triangle, precision=HIGHEST, preferred_element_type=jnp.float32
        )
        mass[var] = summed + mass[var]
    finish(VARS - 1)

    for copy in sum_copies + part_copies:
        copy.wait_send()

    @pl.when(has_left)
    def _():
        for chunk in range(CHUNKS):
            leftward(chunk).wait_send()

    @pl.when(has_right)
    def _():
        for chunk in range(CHUNKS):
            rightward(chunk).wait_send()


def solution(mesh):
    chain, cross = mesh.shape["chain"], mesh.shape["cross"]

    def shards(moments, flags, shifts, fraction):
        row_count, pencils, cells = moments.shape
        assert row_count == ROWS and cells == BLOCK and pencils == BLOCK
        chunk = pltpu.VMEM((CHUNKS, pencils, BLOCK), jnp.float32)
        dma = pltpu.SemaphoreType.DMA
        return pl.pallas_call(
            functools.partial(kernel, chain, cross),
            out_shape=(
                jax.ShapeDtypeStruct(moments.shape, jnp.float32),
                jax.ShapeDtypeStruct((VARS, pencils, cells), jnp.float32),
            ),
            in_specs=[pl.BlockSpec(memory_space=pltpu.HBM)] * 4,
            out_specs=(pl.BlockSpec(memory_space=pltpu.VMEM),) * 2,
            scratch_shapes=[
                pltpu.VMEM(moments.shape, jnp.float32),
                pltpu.VMEM(flags.shape, jnp.int32),
                pltpu.VMEM((1, pencils), jnp.int32),
                pltpu.VMEM((1, pencils), jnp.float32),
                chunk, chunk, chunk, chunk,
                pltpu.VMEM((chain, 8, pencils), jnp.float32),
                pltpu.VMEM((cross, 8, BLOCK), jnp.float32),
                pltpu.VMEM((BLOCK, pencils), jnp.float32),
                pltpu.VMEM((COEFS, pencils, BLOCK), jnp.float32),
                pltpu.VMEM((VARS, pencils, BLOCK), jnp.float32),
                pltpu.VMEM((pencils, BLOCK), jnp.int32),
                pltpu.VMEM((8, BLOCK), jnp.float32),
                pltpu.VMEM((pencils, 2 * BLOCK), jnp.float32),
                dma((CHUNKS,)), dma((CHUNKS,)), dma((CHUNKS,)), dma((CHUNKS,)),
                dma((chain,)), dma((chain,)), dma((cross,)), dma((cross,)), dma((4,)),
            ],
            compiler_params=pltpu.CompilerParams(
                collective_id=0, has_side_effects=True, vmem_limit_bytes=48 << 20
            ),
        )(*(
            pltpu.with_memory_space_constraint(value, pltpu.HBM)
            for value in (moments, flags, shifts.T, fraction.reshape(1, pencils))
        ))

    in_specs = (P(None, "cross", "chain"), P("cross", "chain"), P("cross", "chain"), P("cross"))
    out_specs = (P(None, "cross", "chain"), P(None, "cross", "chain"))
    return jax.shard_map(shards, mesh=mesh, in_specs=in_specs, out_specs=out_specs, check_vma=False)
```

```python
import functools

import jax
import numpy as np
import jax.numpy as jnp
from jax import lax
from jax.experimental import pallas as pl
from jax.experimental.pallas import tpu as pltpu
from jax.sharding import PartitionSpec as P

VARS = 5
MOMENTS = 4
BLOCK = 128
SHIFT_MAX = 48
ROWS = VARS * MOMENTS
STRIDE = SHIFT_MAX + 1
CHUNKS = -(-ROWS * STRIDE // BLOCK)
GROUP = 64
RELAYED = tuple(range(1, CHUNKS, 2))
SEND_SUMS = 2
SUMS_AT = 2
COEFS = 2 * MOMENTS * MOMENTS + MOMENTS
MESH = pl.DeviceIdType.MESH
HIGHEST = lax.Precision.HIGHEST

gauss_nodes = (-0.8611363115940526, -0.3399810435848563, 0.3399810435848563, 0.8611363115940526)
gauss_weights = (0.3478548451374538, 0.6521451548625461, 0.6521451548625461, 0.3478548451374538)


def segments(first, length):
    held = [[] for _ in range(CHUNKS)]
    for row in range(ROWS):
        start = first + STRIDE * row
        chunk, lane = divmod(start, BLOCK)
        held[chunk % CHUNKS].append((lane, row))
        if lane + length > BLOCK:
            held[(chunk + 1) % CHUNKS].append((0, row))
    return [sorted(chunk) for chunk in held]


AFTER_FIRST, AFTER_LENGTH = SHIFT_MAX, SHIFT_MAX + 1
BEFORE_FIRST, BEFORE_LENGTH = 0, SHIFT_MAX
AFTER = segments(AFTER_FIRST, AFTER_LENGTH)
BEFORE = segments(BEFORE_FIRST, BEFORE_LENGTH)


def places(row, first, length):
    chunk, lane = divmod(first + STRIDE * row, BLOCK)
    chunks = [chunk % CHUNKS]
    if lane + length > BLOCK:
        chunks.append((chunk + 1) % CHUNKS)
    return chunks, lane


def last_chunk(var):
    need = [0]
    for row in range(MOMENTS * var, MOMENTS * (var + 1)):
        need += places(row, AFTER_FIRST, AFTER_LENGTH)[0]
        need += places(row, BEFORE_FIRST, BEFORE_LENGTH)[0]
    return max(need)


def legendre_values(point):
    return [
        jnp.ones_like(point),
        point,
        0.5 * (3.0 * point * point - 1.0),
        0.5 * (5.0 * point * point * point - 3.0 * point),
    ]


def interval_matrix(low_end, high_end, offset):
    half = 0.5 * (high_end - low_end)
    middle = 0.5 * (high_end + low_end)
    entries = [[jnp.zeros_like(low_end) for _ in range(4)] for _ in range(4)]
    for node, weight in zip(gauss_nodes, gauss_weights):
        point = middle + half * node
        target = legendre_values(point)
        source = legendre_values(point + offset)
        for k in range(4):
            scaled = weight * half * target[k]
            for m in range(4):
                entries[k][m] = entries[k][m] + scaled * source[m]
    return [(k + 0.5) * entries[k][m] for k in range(4) for m in range(4)]


def partial_weights(fraction):
    shifted = 2.0 * fraction - 1.0
    square = shifted * shifted
    return [
        fraction,
        fraction * fraction - fraction,
        0.25 * (square * shifted - shifted),
        0.5 * (0.5 * (1.25 * square * square - 1.5 * square) + 0.125),
    ]


def corner_relays(mesh):
    ring = np.moveaxis(mesh.devices, mesh.axis_names.index("chain"), 0).reshape(mesh.shape["chain"], -1)[:, 0]
    if any(getattr(device, "coords", None) is None for device in ring):
        return {}, {}
    spots = [tuple(device.coords) for device in ring]
    rightward, leftward = {}, {}
    if len({spot[0] for spot in spots}) == 2 and len({spot[1] for spot in spots}) == 2:
        for index in range(len(spots) - 1):
            low, high = spots[index], spots[index + 1]
            if low[0] != high[0] and low[1] != high[1]:
                for found, source, target, pick in (
                    (rightward, index, index + 1, max), (leftward, index + 1, index, min)
                ):
                    corner = (spots[source][0], spots[target][1])
                    at = [i for i, spot in enumerate(spots) if spot[:2] == corner]
                    if at:
                        found[source] = (pick(at), target)
    return rightward, leftward


def kernel(
    chain, cross, relays,
    moments_in, flags_in, shifts_in, fraction_in,
    remapped, mass,
    moments, flags, shifts, fraction,
    to_left, to_right, from_left, from_right,
    sums, parts, raw, coef, carried, shift_of, mean_of, window,
    relay, left_send, left_recv, right_send, right_recv, relay_send, relay_recv,
    sum_send, sum_recv, part_send, part_recv, input_sem,
):
    pencils = moments.shape[1]
    groups = pencils // GROUP
    me = lax.axis_index("chain")
    plane = lax.axis_index("cross")

    inputs = [
        pltpu.make_async_copy(source, target, input_sem.at[index])
        for index, (source, target) in enumerate(
            ((moments_in, moments), (flags_in, flags), (shifts_in, shifts), (fraction_in, fraction))
        )
    ]
    for copy in inputs:
        copy.start()

    barrier = pltpu.get_barrier_semaphore()
    for step in range(1, chain):
        peer = lax.rem(me + step, chain)
        pl.semaphore_signal(barrier, inc=1, device_id={"chain": peer}, device_id_type=MESH)
    for step in range(1, cross):
        peer = lax.rem(plane + step, cross)
        pl.semaphore_signal(barrier, inc=1, device_id={"cross": peer}, device_id_type=MESH)

    for copy in inputs:
        copy.wait()

    lane = lax.broadcasted_iota(jnp.int32, (GROUP, BLOCK), 1)

    def limited_row(row, rows, keep_linear, keep_full):
        value = moments[row, rows, :]
        order = row % MOMENTS
        if order == 1:
            value = jnp.where(keep_linear, value, 0.0)
        elif order > 1:
            value = jnp.where(keep_full, value, 0.0)
        return value

    def leftward(chunk):
        return pltpu.make_async_remote_copy(
            src_ref=to_left.at[chunk], dst_ref=from_right.at[chunk],
            send_sem=left_send.at[chunk], recv_sem=left_recv.at[chunk],
            device_id={"chain": lax.rem(me + chain - 1, chain)}, device_id_type=MESH,
        )

    def rightward(chunk):
        return pltpu.make_async_remote_copy(
            src_ref=to_right.at[chunk], dst_ref=from_left.at[chunk],
            send_sem=right_send.at[chunk], recv_sem=right_recv.at[chunk],
            device_id={"chain": lax.rem(me + 1, chain)}, device_id_type=MESH,
        )

    has_left, has_right = me > 0, me < chain - 1

    sum_copies = [
        pltpu.make_async_remote_copy(
            src_ref=sums.at[me], dst_ref=sums.at[me],
            send_sem=sum_send.at[step], recv_sem=sum_recv.at[step],
            device_id={"chain": lax.rem(me + step, chain)}, device_id_type=MESH,
        )
        for step in range(1, chain)
    ]

    def send_sums():
        row_id = lax.broadcasted_iota(jnp.int32, (8, BLOCK), 0)
        total = jnp.zeros((8, pencils), jnp.float32)
        for var in range(VARS):
            pick = (row_id == var).astype(jnp.float32)
            total = total + lax.dot_general(
                pick, moments[MOMENTS * var], (((1,), (1,)), ((), ())),
                precision=HIGHEST, preferred_element_type=jnp.float32,
            )
        sums[me] = total
        for copy in sum_copies:
            copy.start()

    def pack(chunk):
        def body(group, carry):
            rows = pl.ds(pl.multiple_of(group * GROUP, GROUP), GROUP)
            flag = flags[rows, :]
            keep_linear, keep_full = flag <= 1, flag == 0
            rolled = {
                row: pltpu.roll(
                    limited_row(row, rows, keep_linear, keep_full),
                    (STRIDE * row + SHIFT_MAX) % BLOCK, 1,
                )
                for row in sorted({row for held in (AFTER, BEFORE) for _, row in held[chunk]})
            }
            for held, target in ((AFTER, to_left), (BEFORE, to_right)):
                value = rolled[held[chunk][0][1]]
                for start, row in held[chunk][1:]:
                    value = jnp.where(lane >= start, rolled[row], value)
                target[chunk, rows, :] = value
            return carry

        lax.fori_loop(0, groups, body, 0)

    right_relays, left_relays = relays

    def to_relay(chunk, source, send_sem, through):
        return pltpu.make_async_remote_copy(
            src_ref=source.at[chunk], dst_ref=relay.at[chunk],
            send_sem=send_sem.at[chunk], recv_sem=relay_recv.at[chunk],
            device_id={"chain": jnp.int32(through)}, device_id_type=MESH,
        )

    def onward(chunk, landing, recv_sem, target):
        return pltpu.make_async_remote_copy(
            src_ref=relay.at[chunk], dst_ref=landing.at[chunk],
            send_sem=relay_send.at[chunk], recv_sem=recv_sem.at[chunk],
            device_id={"chain": jnp.int32(target)}, device_id_type=MESH,
        )

    def send(chunk, direct, wanted, routes, source, send_sem):
        if chunk in RELAYED:
            for start, (through, _) in routes.items():
                wanted = wanted & (me != start)

                @pl.when(me == start)
                def _():
                    to_relay(chunk, source, send_sem, through).start()

        @pl.when(wanted)
        def _():
            direct(chunk).start()

    for chunk in range(CHUNKS):
        pack(chunk)
        if chunk == 0:
            pl.semaphore_wait(barrier, chain - 1 + cross - 1)

        send(chunk, leftward, has_left, left_relays, to_left, left_send)
        send(chunk, rightward, has_right, right_relays, to_right, right_send)

        if chunk == SEND_SUMS - 1:
            send_sums()

    @pl.when(me == 0)
    def _():
        from_left[...] = jnp.zeros_like(from_left)

    @pl.when(me == chain - 1)
    def _():
        from_right[...] = jnp.zeros_like(from_right)

    f = fraction[...]
    first = interval_matrix(-1.0 + 0.0 * f, 1.0 - 2.0 * f, 2.0 * f)
    second = interval_matrix(1.0 - 2.0 * f, 1.0 + 0.0 * f, 2.0 * f - 2.0)
    raw[...] = jnp.zeros_like(raw)
    columns = first + second + partial_weights(f) + [shifts[...].astype(jnp.float32)]
    for index, value in enumerate(columns):
        raw[index : index + 1, :] = value
    turned = jnp.transpose(raw[...])
    for index in range(COEFS):
        coef[index] = jnp.broadcast_to(turned[:, index : index + 1], (pencils, BLOCK))
    shift_of[...] = jnp.broadcast_to(turned[:, COEFS : COEFS + 1], (pencils, BLOCK)).astype(jnp.int32)

    source_cell = lax.broadcasted_iota(jnp.int32, (2 * BLOCK, BLOCK), 0)
    target_cell = lax.broadcasted_iota(jnp.int32, (2 * BLOCK, BLOCK), 1)
    triangle = jnp.where((source_cell < target_cell) | (source_cell >= BLOCK), 1.0, 0.0)

    def halo_row(row, rows, ahead):
        values = []
        for ref, first_lane, length in (
            (from_right, AFTER_FIRST, AFTER_LENGTH),
            (from_left, BEFORE_FIRST, BEFORE_LENGTH),
        ):
            chunks, start = places(row, first_lane, length)
            value = ref[chunks[0], rows, :]
            if len(chunks) > 1:
                value = jnp.where(lane >= start, value, ref[chunks[1], rows, :])
            values.append(value)
        value = jnp.where(ahead, values[0], values[1])
        return pltpu.roll(value, (-(STRIDE * row + SHIFT_MAX)) % BLOCK, 1)

    part_copies = [
        pltpu.make_async_remote_copy(
            src_ref=parts.at[plane], dst_ref=parts.at[plane],
            send_sem=part_send.at[step], recv_sem=part_recv.at[step],
            device_id={"cross": lax.rem(plane + step, cross)}, device_id_type=MESH,
        )
        for step in range(1, cross)
    ]

    def pass_on(chunk):
        for routes, source, send_sem, landing, recv_sem in (
            (right_relays, to_right, right_send, from_left, right_recv),
            (left_relays, to_left, left_send, from_right, left_recv),
        ):
            for through, target in routes.values():

                @pl.when(me == through)
                def _():
                    to_relay(chunk, source, send_sem, through).wait_recv()
                    onward(chunk, landing, recv_sem, target).start()

    def reduce_chain():
        for copy in sum_copies:
            copy.wait_recv()
        before = jnp.zeros((8, pencils), jnp.float32)
        whole = jnp.zeros((8, pencils), jnp.float32)
        for index in range(chain):
            value = sums[index]
            before = before + jnp.where(index < me, value, 0.0)
            whole = whole + value
        parts[plane] = jnp.broadcast_to(jnp.sum(whole, axis=1, keepdims=True), (8, BLOCK))
        for copy in part_copies:
            copy.start()
        raw[0:8, :] = before
        turned = jnp.transpose(raw[...])
        for var in range(VARS):
            carried[var] = jnp.broadcast_to(turned[:, var : var + 1], (pencils, BLOCK))

    def finish_sums():
        for copy in part_copies:
            copy.wait_recv()
        grand = parts[0]
        for index in range(1, cross):
            grand = grand + parts[index]
        mean_of[...] = grand / float(pencils * cross)

    def finish(var):
        mass[var] = (mass[var] + carried[var]) / mean_of[var : var + 1, :]

    ready = 0
    for var in range(VARS):
        for chunk in RELAYED[var:] if var == VARS - 1 else RELAYED[var : var + 1]:
            pass_on(chunk)
        if var == SUMS_AT:
            reduce_chain()
        if var == VARS - 1:
            finish_sums()
            for done in range(VARS - 1):
                finish(done)

        needed = last_chunk(var) + 1
        if needed > ready:
            low, ready = ready, needed

            @pl.when(has_right)
            def _(low=low, high=needed):
                for chunk in range(low, high):
                    leftward(chunk).wait_recv()

            @pl.when(has_left)
            def _(low=low, high=needed):
                for chunk in range(low, high):
                    rightward(chunk).wait_recv()

        def remap(group, carry, var=var):
            rows = pl.ds(pl.multiple_of(group * GROUP, GROUP), GROUP)
            flag = flags[rows, :]
            keep_linear, keep_full = flag <= 1, flag == 0
            shift = shift_of[rows, :]
            ahead = shift >= 0
            turn = shift & (BLOCK - 1)
            outside = jnp.where(ahead, lane - turn, turn - 1 - lane) < 0
            outside_next = jnp.where(ahead, lane - turn - 1, turn - lane) < 0
            at = (lane + turn) & (BLOCK - 1)
            at_next = (lane + turn + 1) & (BLOCK - 1)
            here, beyond = [], []
            for order in range(MOMENTS):
                row = MOMENTS * var + order
                own = limited_row(row, rows, keep_linear, keep_full)
                halo = halo_row(row, rows, ahead)
                here.append(
                    jnp.take_along_axis(
                        jnp.where(outside, halo, own), at, axis=1, mode="promise_in_bounds"
                    )
                )
                beyond.append(
                    jnp.take_along_axis(
                        jnp.where(outside_next, halo, own), at_next, axis=1, mode="promise_in_bounds"
                    )
                )
                if order == 0:
                    gap = jnp.where(outside, jnp.where(ahead, own, -halo), 0.0)
            window[rows, 0:BLOCK] = here[0]
            window[rows, BLOCK : 2 * BLOCK] = gap
            for k in range(MOMENTS):
                value = None
                for m in range(MOMENTS):
                    term = coef[MOMENTS * k + m, rows, :] * here[m]
                    value = term if value is None else value + term
                    value = value + coef[MOMENTS * (MOMENTS + k) + m, rows, :] * beyond[m]
                remapped[MOMENTS * var + k, rows, :] = value
            value = coef[2 * MOMENTS * MOMENTS, rows, :] * here[0]
            for m in range(1, MOMENTS):
                value = value + coef[2 * MOMENTS * MOMENTS + m, rows, :] * here[m]
            mass[var, rows, :] = value
            return carry

        lax.fori_loop(0, groups, remap, 0)
        summed = jnp.dot(
            window[...], triangle, precision=HIGHEST, preferred_element_type=jnp.float32
        )
        mass[var] = summed + mass[var]
    finish(VARS - 1)

    for copy in sum_copies + part_copies:
        copy.wait_send()

    for routes, landing, recv_sem in (
        (right_relays, from_left, right_recv), (left_relays, from_right, left_recv)
    ):
        for through, target in routes.values():

            @pl.when(me == through)
            def _():
                for chunk in RELAYED:
                    onward(chunk, landing, recv_sem, target).wait_send()

    @pl.when(has_left)
    def _():
        for chunk in range(CHUNKS):
            leftward(chunk).wait_send()

    @pl.when(has_right)
    def _():
        for chunk in range(CHUNKS):
            rightward(chunk).wait_send()


def solution(mesh):
    chain, cross = mesh.shape["chain"], mesh.shape["cross"]
    relays = corner_relays(mesh)

    def shards(moments, flags, shifts, fraction):
        row_count, pencils, cells = moments.shape
        assert row_count == ROWS and cells == BLOCK and pencils == BLOCK
        chunk = pltpu.VMEM((CHUNKS, pencils, BLOCK), jnp.float32)
        dma = pltpu.SemaphoreType.DMA
        return pl.pallas_call(
            functools.partial(kernel, chain, cross, relays),
            out_shape=(
                jax.ShapeDtypeStruct(moments.shape, jnp.float32),
                jax.ShapeDtypeStruct((VARS, pencils, cells), jnp.float32),
            ),
            in_specs=[pl.BlockSpec(memory_space=pltpu.HBM)] * 4,
            out_specs=(pl.BlockSpec(memory_space=pltpu.VMEM),) * 2,
            scratch_shapes=[
                pltpu.VMEM(moments.shape, jnp.float32),
                pltpu.VMEM(flags.shape, jnp.int32),
                pltpu.VMEM((1, pencils), jnp.int32),
                pltpu.VMEM((1, pencils), jnp.float32),
                chunk, chunk, chunk, chunk,
                pltpu.VMEM((chain, 8, pencils), jnp.float32),
                pltpu.VMEM((cross, 8, BLOCK), jnp.float32),
                pltpu.VMEM((BLOCK, pencils), jnp.float32),
                pltpu.VMEM((COEFS, pencils, BLOCK), jnp.float32),
                pltpu.VMEM((VARS, pencils, BLOCK), jnp.float32),
                pltpu.VMEM((pencils, BLOCK), jnp.int32),
                pltpu.VMEM((8, BLOCK), jnp.float32),
                pltpu.VMEM((pencils, 2 * BLOCK), jnp.float32),
                chunk, dma((CHUNKS,)), dma((CHUNKS,)), dma((CHUNKS,)), dma((CHUNKS,)),
                dma((CHUNKS,)), dma((CHUNKS,)),
                dma((chain,)), dma((chain,)), dma((cross,)), dma((cross,)), dma((4,)),
            ],
            compiler_params=pltpu.CompilerParams(
                collective_id=0, has_side_effects=True, vmem_limit_bytes=48 << 20
            ),
        )(*(
            pltpu.with_memory_space_constraint(value, pltpu.HBM)
            for value in (moments, flags, shifts.T, fraction.reshape(1, pencils))
        ))

    in_specs = (P(None, "cross", "chain"), P("cross", "chain"), P("cross", "chain"), P("cross"))
    out_specs = (P(None, "cross", "chain"), P(None, "cross", "chain"))
    return jax.shard_map(shards, mesh=mesh, in_specs=in_specs, out_specs=out_specs, check_vma=False)
```

```python
import functools

import jax
import numpy as np
import jax.numpy as jnp
from jax import lax
from jax.experimental import pallas as pl
from jax.experimental.pallas import tpu as pltpu
from jax.sharding import PartitionSpec as P

VARS = 5
MOMENTS = 4
BLOCK = 128
SHIFT_MAX = 48
ROWS = VARS * MOMENTS
STRIDE = SHIFT_MAX + 1
CHUNKS = -(-ROWS * STRIDE // BLOCK)
GROUP = 64
RELAYED = tuple(range(1, CHUNKS, 2))
SEND_SUMS = 2
SUMS_AT = 1
COEFS = 2 * MOMENTS * MOMENTS + MOMENTS
MESH = pl.DeviceIdType.MESH
HIGHEST = lax.Precision.HIGHEST

gauss_nodes = (-0.8611363115940526, -0.3399810435848563, 0.3399810435848563, 0.8611363115940526)
gauss_weights = (0.3478548451374538, 0.6521451548625461, 0.6521451548625461, 0.3478548451374538)


def segments(first, length):
    held = [[] for _ in range(CHUNKS)]
    for row in range(ROWS):
        start = first + STRIDE * row
        chunk, lane = divmod(start, BLOCK)
        held[chunk % CHUNKS].append((lane, row))
        if lane + length > BLOCK:
            held[(chunk + 1) % CHUNKS].append((0, row))
    return [sorted(chunk) for chunk in held]


AFTER_FIRST, AFTER_LENGTH = SHIFT_MAX, SHIFT_MAX + 1
BEFORE_FIRST, BEFORE_LENGTH = 0, SHIFT_MAX
AFTER = segments(AFTER_FIRST, AFTER_LENGTH)
BEFORE = segments(BEFORE_FIRST, BEFORE_LENGTH)


def places(row, first, length):
    chunk, lane = divmod(first + STRIDE * row, BLOCK)
    chunks = [chunk % CHUNKS]
    if lane + length > BLOCK:
        chunks.append((chunk + 1) % CHUNKS)
    return chunks, lane


def last_chunk(var):
    need = [0]
    for row in range(MOMENTS * var, MOMENTS * (var + 1)):
        need += places(row, AFTER_FIRST, AFTER_LENGTH)[0]
        need += places(row, BEFORE_FIRST, BEFORE_LENGTH)[0]
    return max(need)


def legendre_values(point):
    return [
        jnp.ones_like(point),
        point,
        0.5 * (3.0 * point * point - 1.0),
        0.5 * (5.0 * point * point * point - 3.0 * point),
    ]


def interval_matrix(low_end, high_end, offset):
    half = 0.5 * (high_end - low_end)
    middle = 0.5 * (high_end + low_end)
    entries = [[jnp.zeros_like(low_end) for _ in range(4)] for _ in range(4)]
    for node, weight in zip(gauss_nodes, gauss_weights):
        point = middle + half * node
        target = legendre_values(point)
        source = legendre_values(point + offset)
        for k in range(4):
            scaled = weight * half * target[k]
            for m in range(4):
                entries[k][m] = entries[k][m] + scaled * source[m]
    return [(k + 0.5) * entries[k][m] for k in range(4) for m in range(4)]


def partial_weights(fraction):
    shifted = 2.0 * fraction - 1.0
    square = shifted * shifted
    return [
        fraction,
        fraction * fraction - fraction,
        0.25 * (square * shifted - shifted),
        0.5 * (0.5 * (1.25 * square * square - 1.5 * square) + 0.125),
    ]


def corner_relays(mesh):
    ring = np.moveaxis(mesh.devices, mesh.axis_names.index("chain"), 0).reshape(mesh.shape["chain"], -1)[:, 0]
    if any(getattr(device, "coords", None) is None for device in ring):
        return {}, {}
    spots = [tuple(device.coords) for device in ring]
    rightward, leftward = {}, {}
    if len({spot[0] for spot in spots}) == 2 and len({spot[1] for spot in spots}) == 2:
        for index in range(len(spots) - 1):
            low, high = spots[index], spots[index + 1]
            if low[0] != high[0] and low[1] != high[1]:
                for found, source, target, pick in (
                    (rightward, index, index + 1, max), (leftward, index + 1, index, min)
                ):
                    corner = (spots[source][0], spots[target][1])
                    at = [i for i, spot in enumerate(spots) if spot[:2] == corner]
                    if at:
                        found[source] = (pick(at), target)
    return rightward, leftward


def kernel(
    chain, cross, relays,
    moments_in, flags_in, shifts_in, fraction_in,
    remapped, mass,
    moments, flags, shifts, fraction,
    to_left, to_right, from_left, from_right,
    sums, parts, raw, coef, carried, shift_of, mean_of, window,
    relay, left_send, left_recv, right_send, right_recv, relay_send, relay_recv,
    sum_send, sum_recv, part_send, part_recv, input_sem,
):
    pencils = moments.shape[1]
    groups = pencils // GROUP
    me = lax.axis_index("chain")
    plane = lax.axis_index("cross")

    inputs = [
        pltpu.make_async_copy(source, target, input_sem.at[index])
        for index, (source, target) in enumerate(
            ((moments_in, moments), (flags_in, flags), (shifts_in, shifts), (fraction_in, fraction))
        )
    ]
    for copy in inputs:
        copy.start()

    barrier = pltpu.get_barrier_semaphore()
    for step in range(1, chain):
        peer = lax.rem(me + step, chain)
        pl.semaphore_signal(barrier, inc=1, device_id={"chain": peer}, device_id_type=MESH)
    for step in range(1, cross):
        peer = lax.rem(plane + step, cross)
        pl.semaphore_signal(barrier, inc=1, device_id={"cross": peer}, device_id_type=MESH)

    for copy in inputs:
        copy.wait()

    lane = lax.broadcasted_iota(jnp.int32, (GROUP, BLOCK), 1)

    def limited_row(row, rows, keep_linear, keep_full):
        value = moments[row, rows, :]
        order = row % MOMENTS
        if order == 1:
            value = jnp.where(keep_linear, value, 0.0)
        elif order > 1:
            value = jnp.where(keep_full, value, 0.0)
        return value

    def leftward(chunk):
        return pltpu.make_async_remote_copy(
            src_ref=to_left.at[chunk], dst_ref=from_right.at[chunk],
            send_sem=left_send.at[chunk], recv_sem=left_recv.at[chunk],
            device_id={"chain": lax.rem(me + chain - 1, chain)}, device_id_type=MESH,
        )

    def rightward(chunk):
        return pltpu.make_async_remote_copy(
            src_ref=to_right.at[chunk], dst_ref=from_left.at[chunk],
            send_sem=right_send.at[chunk], recv_sem=right_recv.at[chunk],
            device_id={"chain": lax.rem(me + 1, chain)}, device_id_type=MESH,
        )

    has_left, has_right = me > 0, me < chain - 1

    sum_copies = [
        pltpu.make_async_remote_copy(
            src_ref=sums.at[me], dst_ref=sums.at[me],
            send_sem=sum_send.at[step], recv_sem=sum_recv.at[step],
            device_id={"chain": lax.rem(me + step, chain)}, device_id_type=MESH,
        )
        for step in range(1, chain)
    ]

    def send_sums():
        row_id = lax.broadcasted_iota(jnp.int32, (8, BLOCK), 0)
        total = jnp.zeros((8, pencils), jnp.float32)
        for var in range(VARS):
            pick = (row_id == var).astype(jnp.float32)
            total = total + lax.dot_general(
                pick, moments[MOMENTS * var], (((1,), (1,)), ((), ())),
                precision=HIGHEST, preferred_element_type=jnp.float32,
            )
        sums[me] = total
        for copy in sum_copies:
            copy.start()

    def pack(chunk):
        def body(group, carry):
            rows = pl.ds(pl.multiple_of(group * GROUP, GROUP), GROUP)
            flag = flags[rows, :]
            keep_linear, keep_full = flag <= 1, flag == 0
            rolled = {
                row: pltpu.roll(
                    limited_row(row, rows, keep_linear, keep_full),
                    (STRIDE * row + SHIFT_MAX) % BLOCK, 1,
                )
                for row in sorted({row for held in (AFTER, BEFORE) for _, row in held[chunk]})
            }
            for held, target in ((AFTER, to_left), (BEFORE, to_right)):
                value = rolled[held[chunk][0][1]]
                for start, row in held[chunk][1:]:
                    value = jnp.where(lane >= start, rolled[row], value)
                target[chunk, rows, :] = value
            return carry

        lax.fori_loop(0, groups, body, 0)

    right_relays, left_relays = relays

    def to_relay(chunk, source, send_sem, through):
        return pltpu.make_async_remote_copy(
            src_ref=source.at[chunk], dst_ref=relay.at[chunk],
            send_sem=send_sem.at[chunk], recv_sem=relay_recv.at[chunk],
            device_id={"chain": jnp.int32(through)}, device_id_type=MESH,
        )

    def onward(chunk, landing, recv_sem, target):
        return pltpu.make_async_remote_copy(
            src_ref=relay.at[chunk], dst_ref=landing.at[chunk],
            send_sem=relay_send.at[chunk], recv_sem=recv_sem.at[chunk],
            device_id={"chain": jnp.int32(target)}, device_id_type=MESH,
        )

    def send(chunk, direct, wanted, routes, source, send_sem):
        if chunk in RELAYED:
            for start, (through, _) in routes.items():
                wanted = wanted & (me != start)

                @pl.when(me == start)
                def _():
                    to_relay(chunk, source, send_sem, through).start()

        @pl.when(wanted)
        def _():
            direct(chunk).start()

    for chunk in range(CHUNKS):
        pack(chunk)
        if chunk == 0:
            pl.semaphore_wait(barrier, chain - 1 + cross - 1)

        send(chunk, leftward, has_left, left_relays, to_left, left_send)
        send(chunk, rightward, has_right, right_relays, to_right, right_send)

        if chunk == SEND_SUMS - 1:
            send_sums()

    @pl.when(me == 0)
    def _():
        from_left[...] = jnp.zeros_like(from_left)

    @pl.when(me == chain - 1)
    def _():
        from_right[...] = jnp.zeros_like(from_right)

    f = fraction[...]
    first = interval_matrix(-1.0 + 0.0 * f, 1.0 - 2.0 * f, 2.0 * f)
    second = interval_matrix(1.0 - 2.0 * f, 1.0 + 0.0 * f, 2.0 * f - 2.0)
    raw[...] = jnp.zeros_like(raw)
    columns = first + second + partial_weights(f) + [shifts[...].astype(jnp.float32)]
    for index, value in enumerate(columns):
        raw[index : index + 1, :] = value
    turned = jnp.transpose(raw[...])
    for index in range(COEFS):
        coef[index] = jnp.broadcast_to(turned[:, index : index + 1], (pencils, BLOCK))
    shift_of[...] = jnp.broadcast_to(turned[:, COEFS : COEFS + 1], (pencils, BLOCK)).astype(jnp.int32)

    source_cell = lax.broadcasted_iota(jnp.int32, (2 * BLOCK, BLOCK), 0)
    target_cell = lax.broadcasted_iota(jnp.int32, (2 * BLOCK, BLOCK), 1)
    triangle = jnp.where((source_cell < target_cell) | (source_cell >= BLOCK), 1.0, 0.0)

    def halo_row(row, rows, ahead):
        values = []
        for ref, first_lane, length in (
            (from_right, AFTER_FIRST, AFTER_LENGTH),
            (from_left, BEFORE_FIRST, BEFORE_LENGTH),
        ):
            chunks, start = places(row, first_lane, length)
            value = ref[chunks[0], rows, :]
            if len(chunks) > 1:
                value = jnp.where(lane >= start, value, ref[chunks[1], rows, :])
            values.append(value)
        value = jnp.where(ahead, values[0], values[1])
        return pltpu.roll(value, (-(STRIDE * row + SHIFT_MAX)) % BLOCK, 1)

    part_copies = [
        pltpu.make_async_remote_copy(
            src_ref=parts.at[plane], dst_ref=parts.at[plane],
            send_sem=part_send.at[step], recv_sem=part_recv.at[step],
            device_id={"cross": lax.rem(plane + step, cross)}, device_id_type=MESH,
        )
        for step in range(1, cross)
    ]

    def pass_on(chunk):
        for routes, source, send_sem, landing, recv_sem in (
            (right_relays, to_right, right_send, from_left, right_recv),
            (left_relays, to_left, left_send, from_right, left_recv),
        ):
            for through, target in routes.values():

                @pl.when(me == through)
                def _():
                    to_relay(chunk, source, send_sem, through).wait_recv()
                    onward(chunk, landing, recv_sem, target).start()

    def reduce_chain():
        for copy in sum_copies:
            copy.wait_recv()
        before = jnp.zeros((8, pencils), jnp.float32)
        whole = jnp.zeros((8, pencils), jnp.float32)
        for index in range(chain):
            value = sums[index]
            before = before + jnp.where(index < me, value, 0.0)
            whole = whole + value
        parts[plane] = jnp.broadcast_to(jnp.sum(whole, axis=1, keepdims=True), (8, BLOCK))
        for copy in part_copies:
            copy.start()
        raw[0:8, :] = before
        turned = jnp.transpose(raw[...])
        for var in range(VARS):
            carried[var] = jnp.broadcast_to(turned[:, var : var + 1], (pencils, BLOCK))

    def finish_sums():
        for copy in part_copies:
            copy.wait_recv()
        grand = parts[0]
        for index in range(1, cross):
            grand = grand + parts[index]
        mean_of[...] = grand / float(pencils * cross)

    def finish(var):
        mass[var] = (mass[var] + carried[var]) / mean_of[var : var + 1, :]

    ready = 0
    for var in range(VARS):
        for chunk in RELAYED[var:] if var == VARS - 1 else RELAYED[var : var + 1]:
            pass_on(chunk)
        if var == SUMS_AT:
            reduce_chain()
        if var == VARS - 1:
            finish_sums()
            for done in range(VARS - 1):
                finish(done)

        needed = last_chunk(var) + 1
        if needed > ready:
            low, ready = ready, needed

            @pl.when(has_right)
            def _(low=low, high=needed):
                for chunk in range(low, high):
                    leftward(chunk).wait_recv()

            @pl.when(has_left)
            def _(low=low, high=needed):
                for chunk in range(low, high):
                    rightward(chunk).wait_recv()

        def remap(group, carry, var=var):
            rows = pl.ds(pl.multiple_of(group * GROUP, GROUP), GROUP)
            flag = flags[rows, :]
            keep_linear, keep_full = flag <= 1, flag == 0
            shift = shift_of[rows, :]
            ahead = shift >= 0
            turn = shift & (BLOCK - 1)
            outside = jnp.where(ahead, lane - turn, turn - 1 - lane) < 0
            outside_next = jnp.where(ahead, lane - turn - 1, turn - lane) < 0
            at = (lane + turn) & (BLOCK - 1)
            at_next = (lane + turn + 1) & (BLOCK - 1)
            here, beyond = [], []
            for order in range(MOMENTS):
                row = MOMENTS * var + order
                own = limited_row(row, rows, keep_linear, keep_full)
                halo = halo_row(row, rows, ahead)
                here.append(
                    jnp.take_along_axis(
                        jnp.where(outside, halo, own), at, axis=1, mode="promise_in_bounds"
                    )
                )
                beyond.append(
                    jnp.take_along_axis(
                        jnp.where(outside_next, halo, own), at_next, axis=1, mode="promise_in_bounds"
                    )
                )
                if order == 0:
                    gap = jnp.where(outside, jnp.where(ahead, own, -halo), 0.0)
            window[rows, 0:BLOCK] = here[0]
            window[rows, BLOCK : 2 * BLOCK] = gap
            for k in range(MOMENTS):
                value = None
                for m in range(MOMENTS):
                    term = coef[MOMENTS * k + m, rows, :] * here[m]
                    value = term if value is None else value + term
                    value = value + coef[MOMENTS * (MOMENTS + k) + m, rows, :] * beyond[m]
                remapped[MOMENTS * var + k, rows, :] = value
            value = coef[2 * MOMENTS * MOMENTS, rows, :] * here[0]
            for m in range(1, MOMENTS):
                value = value + coef[2 * MOMENTS * MOMENTS + m, rows, :] * here[m]
            mass[var, rows, :] = value
            return carry

        lax.fori_loop(0, groups, remap, 0)
        summed = jnp.dot(
            window[...], triangle, precision=HIGHEST, preferred_element_type=jnp.float32
        )
        mass[var] = summed + mass[var]
    finish(VARS - 1)

    for copy in sum_copies + part_copies:
        copy.wait_send()

    for routes, landing, recv_sem in (
        (right_relays, from_left, right_recv), (left_relays, from_right, left_recv)
    ):
        for through, target in routes.values():

            @pl.when(me == through)
            def _():
                for chunk in RELAYED:
                    onward(chunk, landing, recv_sem, target).wait_send()

    @pl.when(has_left)
    def _():
        for chunk in range(CHUNKS):
            leftward(chunk).wait_send()

    @pl.when(has_right)
    def _():
        for chunk in range(CHUNKS):
            rightward(chunk).wait_send()


def solution(mesh):
    chain, cross = mesh.shape["chain"], mesh.shape["cross"]
    relays = corner_relays(mesh)

    def shards(moments, flags, shifts, fraction):
        row_count, pencils, cells = moments.shape
        assert row_count == ROWS and cells == BLOCK and pencils == BLOCK
        chunk = pltpu.VMEM((CHUNKS, pencils, BLOCK), jnp.float32)
        dma = pltpu.SemaphoreType.DMA
        return pl.pallas_call(
            functools.partial(kernel, chain, cross, relays),
            out_shape=(
                jax.ShapeDtypeStruct(moments.shape, jnp.float32),
                jax.ShapeDtypeStruct((VARS, pencils, cells), jnp.float32),
            ),
            in_specs=[pl.BlockSpec(memory_space=pltpu.HBM)] * 4,
            out_specs=(pl.BlockSpec(memory_space=pltpu.VMEM),) * 2,
            scratch_shapes=[
                pltpu.VMEM(moments.shape, jnp.float32),
                pltpu.VMEM(flags.shape, jnp.int32),
                pltpu.VMEM((1, pencils), jnp.int32),
                pltpu.VMEM((1, pencils), jnp.float32),
                chunk, chunk, chunk, chunk,
                pltpu.VMEM((chain, 8, pencils), jnp.float32),
                pltpu.VMEM((cross, 8, BLOCK), jnp.float32),
                pltpu.VMEM((BLOCK, pencils), jnp.float32),
                pltpu.VMEM((COEFS, pencils, BLOCK), jnp.float32),
                pltpu.VMEM((VARS, pencils, BLOCK), jnp.float32),
                pltpu.VMEM((pencils, BLOCK), jnp.int32),
                pltpu.VMEM((8, BLOCK), jnp.float32),
                pltpu.VMEM((pencils, 2 * BLOCK), jnp.float32),
                chunk, dma((CHUNKS,)), dma((CHUNKS,)), dma((CHUNKS,)), dma((CHUNKS,)),
                dma((CHUNKS,)), dma((CHUNKS,)),
                dma((chain,)), dma((chain,)), dma((cross,)), dma((cross,)), dma((4,)),
            ],
            compiler_params=pltpu.CompilerParams(
                collective_id=0, has_side_effects=True, vmem_limit_bytes=48 << 20
            ),
        )(*(
            pltpu.with_memory_space_constraint(value, pltpu.HBM)
            for value in (moments, flags, shifts.T, fraction.reshape(1, pencils))
        ))

    in_specs = (P(None, "cross", "chain"), P("cross", "chain"), P("cross", "chain"), P("cross"))
    out_specs = (P(None, "cross", "chain"), P(None, "cross", "chain"))
    return jax.shard_map(shards, mesh=mesh, in_specs=in_specs, out_specs=out_specs, check_vma=False)
```
